32 devices in a mesh: seq: 2 (over x), tensor: 4 (over z), server: 4 (over y, core).
Axes of the slice: x: 2, y: 2, z: 4, core: 2. Of those that a mesh axis runs over, the one named last changes fastest.
Arguments:
- queries: bfloat16 [2048, 4096], P(('seq', 'server'), 'tensor'), may hold values from -135 to 135
- keys: bfloat16 [2048, 1024], P(('seq', 'server'), 'tensor'), may hold values from -5 to 5
- values: bfloat16 [2048, 1024], P(('seq', 'server'), 'tensor'), may hold values from -6 to 6
- doc_lengths: int32 [4], replicated, may hold values from 1 to 1024, 2048 in all
- w_out: bfloat16 [4096, 4096], P('tensor'), may hold values from -0.09375 to 0.09375
- d_out: bfloat16 [2048, 4096], P(('seq', 'server')), may hold values from -6 to 6
Outputs:
- attn_out: bfloat16 [2048, 4096], P(('seq', 'server'), 'tensor')
- grad_q: bfloat16 [2048, 4096], P(('seq', 'server'), 'tensor')
- grad_k: bfloat16 [2048, 1024], P(('seq', 'server'), 'tensor')
- grad_v: bfloat16 [2048, 1024], P(('seq', 'server'), 'tensor')
The draws below stay inside these ranges and needn't reach their ends.
Inputs may be any that keep to these rules, and one draw needn't show every extreme that they name: `doc_lengths`: the lengths sum to 2048.
All inputs are finite; a program needn't handle non-finite values.
Results may differ from the reference program's by a relative error of at most 0.025.
Values may be sent and summed in bfloat16 or wider, within the bound.
A program may use at most 128 MiB of HBM per device.

```python
import math
import jax
import jax.numpy as jnp
import numpy as np
from jax import lax

D = 4096
QUERY_HEADS = 32
KEY_VALUE_HEADS = 8
HEAD_SIZE = 128
QUERY_BLOCK_SIZE = 128
PACKED_TOKENS = 2048
DOCUMENT_LIMIT = 1024
NDOC = 4
N_TENSOR = 4


def paired_fields(key):
    seeded = jax.random.fold_in(key, 7151)
    random_key_split, key_query, noise_random_key, key_pick, key_gain = jax.random.split(seeded, 5)
    base_keys = jnp.clip(jax.random.normal(random_key_split, (PACKED_TOKENS, KEY_VALUE_HEADS * HEAD_SIZE), jnp.float32), -4.5, 4.5)
    query_base = jnp.clip(jax.random.normal(key_query, (PACKED_TOKENS, QUERY_HEADS * HEAD_SIZE), jnp.float32), -4.5, 4.5)
    picked = jax.random.randint(key_pick, (PACKED_TOKENS,), 0, 48) == 0
    picked_next = jnp.concatenate([picked[1:], jnp.zeros((1,), jnp.bool_)])
    shifted = jnp.concatenate([base_keys[1:], base_keys[-1:]], axis=0)
    random_noise = jnp.clip(jax.random.normal(noise_random_key, (PACKED_TOKENS, KEY_VALUE_HEADS * HEAD_SIZE), jnp.float32), -3.0, 3.0) * 0.15
    output_keys = jnp.where(picked_next[:, None], jnp.clip(shifted + random_noise, -5.0, 5.0), base_keys)
    strength = jnp.exp(jax.random.uniform(key_gain, (PACKED_TOKENS, QUERY_HEADS), jnp.float32, jnp.log(8.0), jnp.log(26.0)))
    repeated_heads = jnp.repeat(output_keys.reshape(PACKED_TOKENS, KEY_VALUE_HEADS, HEAD_SIZE), QUERY_HEADS // KEY_VALUE_HEADS, axis=1)
    aligned = (strength[:, :, None] * repeated_heads).reshape(PACKED_TOKENS, QUERY_HEADS * HEAD_SIZE)
    query_out = jnp.where(picked[:, None], aligned, query_base)
    return (base_keys, query_base, output_keys, query_out)


def draw_keys(key, part):
    fields = paired_fields(key)
    return fields[0].astype(jnp.bfloat16)


def draw_queries(key, part):
    fields = paired_fields(key)
    return fields[1].astype(jnp.bfloat16)


def block_scale(own_key, extent, cuts, low, top_value):
    def one(dim, parts):
        steps = jax.random.uniform(jax.random.fold_in(jax.random.fold_in(own_key, 6), dim), (parts,), jnp.float32, low / len(cuts), top_value / len(cuts))
        return jnp.repeat(jnp.exp(steps), extent[dim] // parts).reshape((-1,) + (1,) * (len(extent) - dim - 1))

    gain = one(*cuts[0])
    for cut in cuts[1:]:
        gain = gain * one(*cut)
    return gain


def profile(count, total, limit, slope):
    portions = [(1 << 20) // math.isqrt(rank ** slope) + 1 for rank in range(2, count + 1)]
    surplus, counts = total - limit - (count - 1), [1] * (count - 1)
    while surplus > 0:
        candidates = [i for i in range(count - 1) if counts[i] < limit]
        pool, remaining = sum([portions[i] for i in candidates]), surplus
        for i in candidates:
            more = min(limit - counts[i], max(1, remaining * portions[i] // pool), surplus)
            counts[i] = counts[i] + more
            surplus = surplus - more
    return np.array([limit] + counts)


def uneven(stream_key, amount, total, bound, skew):
    if amount == 2:
        one = jax.random.randint(stream_key, (), max(1, total - bound), min(bound, total - 1) + 1)
        return jnp.stack([one, total - one])
    tallies = jnp.asarray(profile(amount, total, bound, skew), jnp.int32)
    couples = (amount - 1) // 2
    donor, sink = tallies[1:1 + 2 * couples:2], tallies[2:2 + 2 * couples:2]
    slack = jnp.minimum(donor - 1, bound - sink)
    moved = jax.random.randint(jax.random.fold_in(stream_key, 1), (couples,), 0, 1 << 20) % (slack + 1)
    tallies = tallies.at[1:1 + 2 * couples:2].set(donor - moved).at[2:2 + 2 * couples:2].set(sink + moved)
    return tallies[jax.random.permutation(jax.random.fold_in(stream_key, 2), amount)]


def bell_draw(stream_key, dims, deviation, bound, shards=(), kind=jnp.bfloat16):
    values = deviation * jax.random.normal(stream_key, dims, jnp.float32)
    if shards:
        values = values * block_scale(stream_key, dims, shards, -0.22, 0.18)
    return jnp.clip(values, -bound, bound).astype(kind)


def setup_inputs(seed: int = 0) -> dict:
    splits = jax.random.split(jax.random.key(seed), 7)
    return {
        "queries": draw_queries(jax.random.fold_in(splits[6], 71), 0),
        "keys": draw_keys(jax.random.fold_in(splits[6], 71), 0),
        "values": bell_draw(splits[2], (PACKED_TOKENS, KEY_VALUE_HEADS * HEAD_SIZE), 1.0, 6.0, ((0, 8), (1, 4))),
        "doc_lengths": uneven(splits[3], NDOC, PACKED_TOKENS, DOCUMENT_LIMIT, 2).astype(jnp.int32),
        "w_out": bell_draw(splits[4], (QUERY_HEADS * HEAD_SIZE, D), (QUERY_HEADS * HEAD_SIZE) ** -0.5, 0.09375, ((0, 4),)),
        "d_out": bell_draw(splits[5], (PACKED_TOKENS, D), 1.0, 6.0, ((0, 8),)),
    }


def segment_ids(positions, doc_ends):
    return jnp.sum((doc_ends[None, :] <= positions[:, None]).astype(jnp.int32), axis=1)


def reference(queries, keys, values, doc_lengths, w_out, d_out):
    doc_ends = jnp.cumsum(doc_lengths).astype(jnp.int32)
    queries_per_key_head = QUERY_HEADS // KEY_VALUE_HEADS
    window_span = DOCUMENT_LIMIT + QUERY_BLOCK_SIZE
    scale_factor = HEAD_SIZE ** -0.5
    n_blocks = PACKED_TOKENS // QUERY_BLOCK_SIZE
    highest_precision = lax.Precision.HIGHEST
    padding_rows = jnp.zeros((DOCUMENT_LIMIT, KEY_VALUE_HEADS * HEAD_SIZE), keys.dtype)
    padded_keys = jnp.concatenate([padding_rows, keys], axis=0)
    padded_values = jnp.concatenate([padding_rows, values], axis=0)
    attention_gradient = lax.dot_general(d_out, w_out, (((1,), (1,)), ((), ())), preferred_element_type=jnp.float32).astype(jnp.bfloat16)

    def one_block(running, block_index):
        grad_k_acc, grad_v_acc = running
        anchor_point = (block_index * QUERY_BLOCK_SIZE).astype(jnp.int32)
        q_pos = anchor_point + jnp.arange(QUERY_BLOCK_SIZE, dtype=jnp.int32)
        k_pos = anchor_point - DOCUMENT_LIMIT + jnp.arange(window_span, dtype=jnp.int32)
        allowed = (k_pos[None, :] >= 0) & (k_pos[None, :] <= q_pos[:, None]) & (segment_ids(k_pos, doc_ends)[None, :] == segment_ids(q_pos, doc_ends)[:, None])
        query_block = lax.dynamic_slice_in_dim(queries, anchor_point, QUERY_BLOCK_SIZE, 0).astype(jnp.float32).reshape(QUERY_BLOCK_SIZE, KEY_VALUE_HEADS, queries_per_key_head, HEAD_SIZE)
        key_window = lax.dynamic_slice_in_dim(padded_keys, anchor_point, window_span, 0).astype(jnp.float32).reshape(window_span, KEY_VALUE_HEADS, HEAD_SIZE)
        value_window = lax.dynamic_slice_in_dim(padded_values, anchor_point, window_span, 0).astype(jnp.float32).reshape(window_span, KEY_VALUE_HEADS, HEAD_SIZE)
        output_gradient_block = lax.dynamic_slice_in_dim(attention_gradient, anchor_point, QUERY_BLOCK_SIZE, 0).astype(jnp.float32).reshape(QUERY_BLOCK_SIZE, KEY_VALUE_HEADS, queries_per_key_head, HEAD_SIZE)
        scores = jnp.einsum("tgrd,kgd->grtk", query_block, key_window, precision=highest_precision) * scale_factor
        masked = jnp.where(allowed, scores, -jnp.inf)
        row_top = jnp.max(masked, axis=-1, keepdims=True)
        weights = jnp.exp(masked - row_top)
        shares = weights / jnp.sum(weights, axis=-1, keepdims=True)
        lower_shares = lax.optimization_barrier(shares.astype(jnp.bfloat16)).astype(jnp.float32)
        attn_blk = jnp.einsum("grtk,kgd->tgrd", lower_shares, value_window, precision=highest_precision).astype(jnp.bfloat16)
        attn_back = lax.optimization_barrier(attn_blk).astype(jnp.float32)
        row_delta = jnp.transpose(jnp.sum(attn_back * output_gradient_block, axis=-1), (1, 2, 0))[..., None]
        d_shares = jnp.einsum("tgrd,kgd->grtk", output_gradient_block, value_window, precision=highest_precision)
        score_gradient = lax.optimization_barrier((shares * (d_shares - row_delta)).astype(jnp.bfloat16)).astype(jnp.float32)
        grad_q_blk = (jnp.einsum("grtk,kgd->tgrd", score_gradient, key_window, precision=highest_precision) * scale_factor).astype(jnp.bfloat16)
        partial_key = (jnp.einsum("acul,uacz->laz", score_gradient, query_block, precision=highest_precision) * scale_factor).reshape(window_span, KEY_VALUE_HEADS * HEAD_SIZE)
        partial_value_rows = jnp.einsum("acul,uacz->laz", lower_shares, output_gradient_block, precision=highest_precision).reshape(window_span, KEY_VALUE_HEADS * HEAD_SIZE)
        grad_k_acc = lax.dynamic_update_slice_in_dim(grad_k_acc, lax.dynamic_slice_in_dim(grad_k_acc, anchor_point, window_span, 0) + partial_key, anchor_point, 0)
        grad_v_acc = lax.dynamic_update_slice_in_dim(grad_v_acc, lax.dynamic_slice_in_dim(grad_v_acc, anchor_point, window_span, 0) + partial_value_rows, anchor_point, 0)
        return (grad_k_acc, grad_v_acc), (attn_blk.reshape(QUERY_BLOCK_SIZE, QUERY_HEADS * HEAD_SIZE), grad_q_blk.reshape(QUERY_BLOCK_SIZE, QUERY_HEADS * HEAD_SIZE))

    zero_accumulator = jnp.zeros((PACKED_TOKENS + DOCUMENT_LIMIT, KEY_VALUE_HEADS * HEAD_SIZE), jnp.float32)
    finals, stacked = lax.scan(one_block, (zero_accumulator, zero_accumulator), jnp.arange(n_blocks, dtype=jnp.int32))
    attn = stacked[0].reshape(PACKED_TOKENS, QUERY_HEADS * HEAD_SIZE)
    grad_q = stacked[1].reshape(PACKED_TOKENS, QUERY_HEADS * HEAD_SIZE)
    group_width = QUERY_HEADS * HEAD_SIZE // N_TENSOR
    summed = jnp.zeros((PACKED_TOKENS, D), jnp.float32)
    for shard_index in range(N_TENSOR):
        row_begin = shard_index * group_width
        partial_value = jnp.dot(attn[:, row_begin:row_begin + group_width], w_out[row_begin:row_begin + group_width], preferred_element_type=jnp.float32)
        summed = summed + lax.optimization_barrier(partial_value.astype(jnp.bfloat16)).astype(jnp.float32)
    attn_out = summed.astype(jnp.bfloat16)
    grad_k = finals[0][DOCUMENT_LIMIT:].astype(jnp.bfloat16)
    grad_v = finals[1][DOCUMENT_LIMIT:].astype(jnp.bfloat16)
    return attn_out, grad_q, grad_k, grad_v
```

```python
import functools
import math

import jax
import jax.numpy as jnp
from jax import lax
from jax.experimental import pallas as pl
from jax.experimental.pallas import tpu as pltpu
from jax.sharding import PartitionSpec as P

HEAD = 128
REACH = 4
CHUNKS = 2
ROW_BLOCK = 32
MESH = pl.DeviceIdType.MESH
NT = (((1,), (1,)), ((), ()))
TN = (((0,), (0,)), ((), ()))


def dot(a, b, dims=(((1,), (0,)), ((), ()))):
    return lax.dot_general(a, b, dims, preferred_element_type=jnp.float32)


def kernel(
    sizes,
    q_hbm, k_hbm, v_hbm, doc, w_hbm, do_hbm,
    out_ref, gq_ref, gk_ref, gv_ref,
    q_in, do_in, w, kx, vx, qs, dos, attn, bias, s_ref, p_ref, delta,
    dp_ref, ds_ref, dq_acc, gsk, gsv, grk, grv, gown, part, rr, rl,
    loc_sem, w_sem, kv_send, kv_recv, fw_send, fw_recv, g_send, g_recv,
    r_send, r_recv, l_send, l_recv,
):
    n_seq, n_server, n_t = sizes
    n_shards = n_seq * n_server
    rows = q_in.shape[0]
    heads = q_in.shape[1] // HEAD
    groups = kx.shape[1] // HEAD
    per = heads // groups
    chunk = rows // CHUNKS
    ext = kx.shape[0]
    reach_rows = REACH * rows
    window = reach_rows + chunk
    crows = per * chunk
    width = out_ref.shape[1]
    scale = HEAD ** -0.5

    shard = lax.axis_index("seq") * n_server + lax.axis_index("server")
    t = lax.axis_index("tensor")

    def at_shard(other):
        return {"seq": other // n_server, "server": lax.rem(other, n_server)}

    loads = [
        pltpu.make_async_copy(k_hbm, kx.at[pl.ds(reach_rows, rows)], loc_sem.at[0]),
        pltpu.make_async_copy(v_hbm, vx.at[pl.ds(reach_rows, rows)], loc_sem.at[1]),
        pltpu.make_async_copy(do_hbm, do_in, loc_sem.at[2]),
        pltpu.make_async_copy(q_hbm, q_in, loc_sem.at[3]),
    ]
    n_w = w_sem.shape[0]
    w_rows = w.shape[0] // n_w
    w_loads = [
        pltpu.make_async_copy(
            w_hbm.at[pl.ds(j * w_rows, w_rows)], w.at[pl.ds(j * w_rows, w_rows)], w_sem.at[j]
        )
        for j in range(n_w)
    ]
    for c in loads:
        c.start()
    for c in w_loads:
        c.start()

    barrier = pltpu.get_barrier_semaphore()
    count = jnp.int32(0)
    for step in range(1, REACH + 1):
        for sign in (1, -1):
            other = shard + sign * step
            ok = (other >= 0) & (other < n_shards)

            @pl.when(ok)
            def _():
                pl.semaphore_signal(barrier, inc=1, device_id=at_shard(other), device_id_type=MESH)

            count = count + ok.astype(jnp.int32)
    for sign in (1, -1):
        other = t + sign
        ok = (other >= 0) & (other < n_t)

        @pl.when(ok)
        def _():
            pl.semaphore_signal(barrier, inc=1, device_id={"tensor": other}, device_id_type=MESH)

        count = count + ok.astype(jnp.int32)
    pl.semaphore_wait(barrier, count)

    def slot(distance):
        return pl.ds((REACH - distance) * rows, rows)

    def kv_copy(i, distance):
        src, dst = ((k_hbm, kx), (v_hbm, vx))[i]
        e = 2 * (distance // 2 - 1) + i
        return pltpu.make_async_remote_copy(
            src_ref=src,
            dst_ref=dst.at[slot(distance)],
            send_sem=kv_send.at[e],
            recv_sem=kv_recv.at[e],
            device_id=at_shard(shard + distance),
            device_id_type=MESH,
        )

    even = lax.rem(shard, 2) == 0
    partner = shard + 1 - 2 * lax.rem(shard, 2)

    def fw_copy(i, from_distance, to_distance):
        ref = (kx, vx)[i]
        e = 2 * (to_distance // 2) + i
        return pltpu.make_async_remote_copy(
            src_ref=ref.at[slot(from_distance)],
            dst_ref=ref.at[slot(to_distance)],
            send_sem=fw_send.at[e],
            recv_sem=fw_recv.at[e],
            device_id=at_shard(partner),
            device_id_type=MESH,
        )

    for distance in (4, 2):

        @pl.when(shard + distance < n_shards)
        def _():
            for i in range(2):
                kv_copy(i, distance).start()

    for c in loads[:2]:
        c.wait()

    @pl.when(even)
    def _():
        for i in range(2):
            fw_copy(i, 0, 1).start()

    for distance in range(1, REACH + 1):

        @pl.when(shard < distance)
        def _():
            kx[slot(distance)] = jnp.zeros((rows, kx.shape[1]), kx.dtype)
            vx[slot(distance)] = jnp.zeros((rows, kx.shape[1]), kx.dtype)

    loads[2].wait()
    loads[3].wait()
    heads_per_w = w_rows // HEAD
    for j in range(n_w):
        w_loads[j].wait()
        d = dot(do_in[...], w[pl.ds(j * w_rows, w_rows)], NT).astype(jnp.bfloat16)
        for a in range(heads_per_w):
            h = j * heads_per_w + a
            g, r = h // per, h % per
            for c in range(CHUNKS):
                place = pl.ds(c * crows + r * chunk, chunk)
                dos[g, place] = d[c * chunk : (c + 1) * chunk, a * HEAD : (a + 1) * HEAD]
                qs[g, place] = q_in[pl.ds(c * chunk, chunk), pl.ds(h * HEAD, HEAD)]

    for c in range(CHUNKS):
        first = shard * rows + c * chunk
        q_pos = first + lax.broadcasted_iota(jnp.int32, (chunk, 1), 0)
        start = jnp.zeros((chunk, 1), jnp.int32)
        end = jnp.int32(0)
        for a in range(doc.shape[0]):
            end = end + doc[a]
            start = jnp.maximum(start, jnp.where(end <= q_pos, end, 0))
        k_pos = first - reach_rows + lax.broadcasted_iota(jnp.int32, (chunk, window), 1)
        bias[c] = jnp.where((k_pos >= start) & (k_pos <= q_pos), 0.0, -1e30).astype(jnp.float32)
    if CHUNKS > 1:
        for g in range(groups):
            for c in range(CHUNKS):
                place = pl.ds(c * crows, crows)
                if c > 0:
                    p_ref[g, place, pl.ds(0, c * chunk)] = jnp.zeros((crows, c * chunk), jnp.bfloat16)
                tail = ext - window - c * chunk
                if tail > 0:
                    p_ref[g, place, pl.ds(ext - tail, tail)] = jnp.zeros((crows, tail), jnp.bfloat16)

    @pl.when(shard >= 2)
    def _():
        for i in range(2):
            kv_copy(i, 2).wait_recv()

        @pl.when(even)
        def _():
            for i in range(2):
                fw_copy(i, 2, 3).start()

        @pl.when(jnp.logical_not(even))
        def _():
            for i in range(2):
                fw_copy(i, 2, 1).start()

    @pl.when(shard >= 4)
    def _():
        for i in range(2):
            kv_copy(i, 4).wait_recv()

        @pl.when(jnp.logical_not(even))
        def _():
            for i in range(2):
                fw_copy(i, 4, 3).start()

    @pl.when(shard >= 1)
    def _():
        for i in range(2):
            fw_copy(i, 0, 1).wait_recv()

    @pl.when(shard >= 3)
    def _():
        for i in range(2):
            fw_copy(i, 2, 3).wait_recv()

    order = []
    for a in range((n_t + 1) // 2):
        order.append(n_t - 1 - a)
        if a != n_t - 1 - a:
            order.append(a)

    def cols(d):
        return pl.ds(d * width, width)

    def right_copy(c, d):
        return pltpu.make_async_remote_copy(
            src_ref=part.at[c, d],
            dst_ref=rr.at[c, d],
            send_sem=r_send.at[c, d],
            recv_sem=r_recv.at[c, d],
            device_id={"tensor": t + 1},
            device_id_type=MESH,
        )

    def left_copy(c, d):
        return pltpu.make_async_remote_copy(
            src_ref=part.at[c, d],
            dst_ref=rl.at[c, d],
            send_sem=l_send.at[c, d],
            recv_sem=l_recv.at[c, d],
            device_id={"tensor": t - 1},
            device_id_type=MESH,
        )

    def relay(c, d):
        e = n_t - 1 - d
        if d > 0:

            @pl.when((t > 0) & (t < d))
            def _():
                right_copy(c, d).wait_recv()
                part[c, d] = (part[c, d].astype(jnp.float32) + rr[c, d].astype(jnp.float32)).astype(
                    jnp.bfloat16
                )
                right_copy(c, d).start()

            @pl.when((t < n_t - 1) & (t > e))
            def _():
                left_copy(c, e).wait_recv()
                part[c, e] = (part[c, e].astype(jnp.float32) + rl[c, e].astype(jnp.float32)).astype(
                    jnp.bfloat16
                )
                left_copy(c, e).start()

    factor = scale * math.log2(math.e)
    blocks = crows // ROW_BLOCK
    per_head = chunk // ROW_BLOCK
    for c in range(CHUNKS):
        place = pl.ds(c * crows, crows)
        win = pl.ds(c * chunk, window)
        for g in range(groups):
            gc = pl.ds(g * HEAD, HEAD)
            s_ref[...] = dot(qs[g, place], kx[win, gc], NT)

            @pl.loop(0, blocks, unroll=2)
            def _(b):
                row = pl.multiple_of(b * ROW_BLOCK, ROW_BLOCK)
                brow = pl.multiple_of(lax.rem(b, per_head) * ROW_BLOCK, ROW_BLOCK)
                s = s_ref[pl.ds(row, ROW_BLOCK)] + bias[c, pl.ds(brow, ROW_BLOCK)]
                top = jnp.max(s, axis=1, keepdims=True)
                e = jnp.exp2((s - top) * factor)
                inv = 1.0 / jnp.sum(e, axis=1, keepdims=True)
                p_ref[g, pl.ds(c * crows + row, ROW_BLOCK), win] = (e * inv).astype(jnp.bfloat16)

            o = dot(p_ref[g, place, win], vx[win, gc]).astype(jnp.bfloat16)
            delta[g, place] = jnp.sum(
                o.astype(jnp.float32) * dos[g, place].astype(jnp.float32), axis=1, keepdims=True
            )
            for r in range(per):
                attn[c, :, pl.ds((g * per + r) * HEAD, HEAD)] = o[r * chunk : (r + 1) * chunk]
        for d in order:
            part[c, d] = dot(attn[c], w[:, cols(d)]).astype(jnp.bfloat16)
            if d > 0:

                @pl.when(t == 0)
                def _():
                    right_copy(c, d).start()

            if d < n_t - 1:

                @pl.when(t == n_t - 1)
                def _():
                    left_copy(c, d).start()

    def grad_copy(i, distance):
        src, dst = ((gsk, grk), (gsv, grv))[i]
        return pltpu.make_async_remote_copy(
            src_ref=src.at[distance - 1],
            dst_ref=dst.at[distance - 1],
            send_sem=g_send.at[i, distance - 1],
            recv_sem=g_recv.at[i, distance - 1],
            device_id=at_shard(shard - distance),
            device_id_type=MESH,
        )

    for kb in range(REACH + 1):
        distance = REACH - kb
        keys = pl.ds(kb * rows, rows)
        for g in range(groups):
            gc = pl.ds(g * HEAD, HEAD)
            dp_ref[...] = dot(dos[g], vx[keys, gc], NT)
            ds_ref[...] = (p_ref[g, :, keys].astype(jnp.float32) * (dp_ref[...] - delta[g])).astype(
                jnp.bfloat16
            )
            dq = dot(ds_ref[...], kx[keys, gc])
            if kb == 0:
                dq_acc[g] = dq
            else:
                dq_acc[g] += dq
            dk = dot(ds_ref[...], qs[g], TN) * scale
            dv = dot(p_ref[g, :, keys], dos[g], TN)
            if distance > 0:
                gsk[distance - 1, :, gc] = dk.astype(jnp.bfloat16)
                gsv[distance - 1, :, gc] = dv.astype(jnp.bfloat16)
            else:
                gown[0, :, gc] = dk
                gown[1, :, gc] = dv
        if distance > 0:

            @pl.when(shard >= distance)
            def _():
                for i in range(2):
                    grad_copy(i, distance).start()

        if kb == 2:
            relay(0, n_t - 1)
        if kb == 4:
            for d in range(n_t - 2, 0, -1):
                relay(0, d)

    for g in range(groups):
        for c in range(CHUNKS):
            for r in range(per):
                gq_ref[pl.ds(c * chunk, chunk), pl.ds((g * per + r) * HEAD, HEAD)] = (
                    dq_acc[g, pl.ds(c * crows + r * chunk, chunk)] * scale
                ).astype(jnp.bfloat16)

    for c in range(1, CHUNKS):
        for d in range(n_t - 1, 0, -1):
            relay(c, d)

    for distance in range(REACH, 0, -1):

        @pl.when(shard + distance < n_shards)
        def _():
            for i, ref in enumerate((grk, grv)):
                grad_copy(i, distance).wait_recv()
                gown[i] += ref[distance - 1].astype(jnp.float32)

    gk_ref[...] = gown[0].astype(jnp.bfloat16)
    gv_ref[...] = gown[1].astype(jnp.bfloat16)

    for c in range(CHUNKS):
        here = pl.ds(c * chunk, chunk)
        for d in range(n_t):

            @pl.when(t == d)
            def _():
                total = part[c, d].astype(jnp.float32)
                if d > 0:
                    right_copy(c, d).wait_recv()
                    total = total + rr[c, d].astype(jnp.float32)
                if d < n_t - 1:
                    left_copy(c, d).wait_recv()
                    total = total + rl[c, d].astype(jnp.float32)
                out_ref[here] = total.astype(jnp.bfloat16)

    for distance in (4, 2):

        @pl.when(shard + distance < n_shards)
        def _():
            for i in range(2):
                kv_copy(i, distance).wait_send()

    for i in range(2):

        @pl.when(even)
        def _():
            fw_copy(i, 0, 1).wait_send()

        @pl.when(even & (shard >= 2))
        def _():
            fw_copy(i, 2, 3).wait_send()

        @pl.when(jnp.logical_not(even) & (shard >= 2))
        def _():
            fw_copy(i, 2, 1).wait_send()

        @pl.when(jnp.logical_not(even) & (shard >= 4))
        def _():
            fw_copy(i, 4, 3).wait_send()

        for distance in range(1, REACH + 1):

            @pl.when(shard >= distance)
            def _():
                grad_copy(i, distance).wait_send()

    for c in range(CHUNKS):
        for d in range(n_t):

            @pl.when(t < d)
            def _():
                right_copy(c, d).wait_send()

            @pl.when(t > d)
            def _():
                left_copy(c, d).wait_send()


def shards(sizes, queries, keys, values, doc_lengths, w_out, d_out):
    n_t = sizes[2]
    rows, q_width = queries.shape
    kv_width = keys.shape[1]
    groups = kv_width // HEAD
    heads = q_width // HEAD
    per = heads // groups
    chunk = rows // CHUNKS
    ext = (REACH + 1) * rows
    window = REACH * rows + chunk
    d_model = w_out.shape[1]
    width = d_model // n_t
    bf, f32 = jnp.bfloat16, jnp.float32
    all_rows = per * rows
    n_w = 4
    anywhere = pl.BlockSpec(memory_space=pl.ANY)
    vmem = pl.BlockSpec(memory_space=pltpu.VMEM)
    dma = pltpu.SemaphoreType.DMA
    return pl.pallas_call(
        functools.partial(kernel, sizes),
        out_shape=(
            jax.ShapeDtypeStruct((rows, width), bf),
            jax.ShapeDtypeStruct((rows, q_width), bf),
            jax.ShapeDtypeStruct((rows, kv_width), bf),
            jax.ShapeDtypeStruct((rows, kv_width), bf),
        ),
        in_specs=[
            anywhere, anywhere, anywhere, pl.BlockSpec(memory_space=pltpu.SMEM), anywhere, anywhere,
        ],
        out_specs=(vmem,) * 4,
        scratch_shapes=[
            pltpu.VMEM((rows, q_width), bf),
            pltpu.VMEM((rows, d_model), bf),
            pltpu.VMEM(w_out.shape, bf),
            pltpu.VMEM((ext, kv_width), bf),
            pltpu.VMEM((ext, kv_width), bf),
            pltpu.VMEM((groups, all_rows, HEAD), bf),
            pltpu.VMEM((groups, all_rows, HEAD), bf),
            pltpu.VMEM((CHUNKS, chunk, q_width), bf),
            pltpu.VMEM((CHUNKS, chunk, window), f32),
            pltpu.VMEM((per * chunk, window), f32),
            pltpu.VMEM((groups, all_rows, ext), bf),
            pltpu.VMEM((groups, all_rows, 1), f32),
            pltpu.VMEM((all_rows, rows), f32),
            pltpu.VMEM((all_rows, rows), bf),
            pltpu.VMEM((groups, all_rows, HEAD), f32),
            pltpu.VMEM((REACH, rows, kv_width), bf),
            pltpu.VMEM((REACH, rows, kv_width), bf),
            pltpu.VMEM((REACH, rows, kv_width), bf),
            pltpu.VMEM((REACH, rows, kv_width), bf),
            pltpu.VMEM((2, rows, kv_width), f32),
            pltpu.VMEM((CHUNKS, n_t, chunk, width), bf),
            pltpu.VMEM((CHUNKS, n_t, chunk, width), bf),
            pltpu.VMEM((CHUNKS, n_t, chunk, width), bf),
            dma((4,)),
            dma((n_w,)),
            dma((4,)),
            dma((4,)),
            dma((4,)),
            dma((4,)),
            dma((2, REACH)),
            dma((2, REACH)),
            dma((CHUNKS, n_t)),
            dma((CHUNKS, n_t)),
            dma((CHUNKS, n_t)),
            dma((CHUNKS, n_t)),
        ],
        compiler_params=pltpu.CompilerParams(
            collective_id=0, has_side_effects=True, vmem_limit_bytes=60 * 1024 * 1024
        ),
        name="layer",
    )(queries, keys, values, doc_lengths, w_out, d_out)


def solution(mesh):
    sizes = tuple(mesh.shape[a] for a in ("seq", "server", "tensor"))
    tokens = P(("seq", "server"), "tensor")
    return jax.shard_map(
        functools.partial(shards, sizes),
        mesh=mesh,
        in_specs=(tokens, tokens, tokens, P(), P("tensor", None), P(("seq", "server"), None)),
        out_specs=(tokens,) * 4,
        check_vma=False,
    )
```

```python
import functools
import math

import jax
import jax.numpy as jnp
from jax import lax
from jax.experimental import pallas as pl
from jax.experimental.pallas import tpu as pltpu
from jax.sharding import PartitionSpec as P

HEAD = 128
REACH = 4
CHUNKS = 2
ROW_BLOCK = 32
MESH = pl.DeviceIdType.MESH
NT = (((1,), (1,)), ((), ()))
TN = (((0,), (0,)), ((), ()))


def dot(a, b, dims=(((1,), (0,)), ((), ()))):
    return lax.dot_general(a, b, dims, preferred_element_type=jnp.float32)


def kernel(
    sizes,
    q_hbm, k_hbm, v_hbm, doc, w_hbm, do_hbm,
    out_ref, gq_ref, gk_ref, gv_ref,
    q_in, do_in, w, kx, vx, qs, dos, attn, bias, s_ref, p_ref, delta,
    dp_ref, ds_ref, dq_acc, gsk, gsv, gpk, gpv, grk, grv, gown, part, rr, rl,
    loc_sem, w_sem, kv_send, kv_recv, fw_send, fw_recv, p_send, p_recv, g_send, g_recv,
    r_send, r_recv, l_send, l_recv,
):
    n_seq, n_server, n_t = sizes
    n_shards = n_seq * n_server
    rows = q_in.shape[0]
    heads = q_in.shape[1] // HEAD
    groups = kx.shape[1] // HEAD
    per = heads // groups
    chunk = rows // CHUNKS
    ext = kx.shape[0]
    reach_rows = REACH * rows
    window = reach_rows + chunk
    crows = per * chunk
    width = out_ref.shape[1]
    scale = HEAD ** -0.5

    shard = lax.axis_index("seq") * n_server + lax.axis_index("server")
    t = lax.axis_index("tensor")

    def at_shard(other):
        return {"seq": other // n_server, "server": lax.rem(other, n_server)}

    loads = [
        pltpu.make_async_copy(k_hbm, kx.at[pl.ds(reach_rows, rows)], loc_sem.at[0]),
        pltpu.make_async_copy(v_hbm, vx.at[pl.ds(reach_rows, rows)], loc_sem.at[1]),
        pltpu.make_async_copy(do_hbm, do_in, loc_sem.at[2]),
        pltpu.make_async_copy(q_hbm, q_in, loc_sem.at[3]),
    ]
    n_w = w_sem.shape[0]
    w_rows = w.shape[0] // n_w
    w_loads = [
        pltpu.make_async_copy(
            w_hbm.at[pl.ds(j * w_rows, w_rows)], w.at[pl.ds(j * w_rows, w_rows)], w_sem.at[j]
        )
        for j in range(n_w)
    ]
    for c in loads:
        c.start()
    for c in w_loads:
        c.start()

    barrier = pltpu.get_barrier_semaphore()
    count = jnp.int32(0)
    partner = shard + 1 - 2 * lax.rem(shard, 2)
    pl.semaphore_signal(barrier, inc=1, device_id=at_shard(partner), device_id_type=MESH)
    count = count + 1
    for step in (2, 4):
        for sign in (1, -1):
            other = shard + sign * step
            ok = (other >= 0) & (other < n_shards)

            @pl.when(ok)
            def _():
                pl.semaphore_signal(barrier, inc=1, device_id=at_shard(other), device_id_type=MESH)

            count = count + ok.astype(jnp.int32)
    for sign in (1, -1):
        other = t + sign
        ok = (other >= 0) & (other < n_t)

        @pl.when(ok)
        def _():
            pl.semaphore_signal(barrier, inc=1, device_id={"tensor": other}, device_id_type=MESH)

        count = count + ok.astype(jnp.int32)
    pl.semaphore_wait(barrier, count)

    def slot(distance):
        return pl.ds((REACH - distance) * rows, rows)

    def kv_copy(i, distance):
        src, dst = ((k_hbm, kx), (v_hbm, vx))[i]
        e = 2 * (distance // 2 - 1) + i
        return pltpu.make_async_remote_copy(
            src_ref=src,
            dst_ref=dst.at[slot(distance)],
            send_sem=kv_send.at[e],
            recv_sem=kv_recv.at[e],
            device_id=at_shard(shard + distance),
            device_id_type=MESH,
        )

    even = lax.rem(shard, 2) == 0

    def fw_copy(i, from_distance, to_distance):
        ref = (kx, vx)[i]
        e = 2 * (to_distance // 2) + i
        return pltpu.make_async_remote_copy(
            src_ref=ref.at[slot(from_distance)],
            dst_ref=ref.at[slot(to_distance)],
            send_sem=fw_send.at[e],
            recv_sem=fw_recv.at[e],
            device_id=at_shard(partner),
            device_id_type=MESH,
        )

    for i in range(2):
        for distance in (4, 2):

            @pl.when(shard + distance < n_shards)
            def _():
                kv_copy(i, distance).start()

    for c in loads[:2]:
        c.wait()

    @pl.when(even)
    def _():
        for i in range(2):
            fw_copy(i, 0, 1).start()

    for distance in range(1, REACH + 1):

        @pl.when(shard < distance)
        def _():
            kx[slot(distance)] = jnp.zeros((rows, kx.shape[1]), kx.dtype)
            vx[slot(distance)] = jnp.zeros((rows, kx.shape[1]), kx.dtype)

    loads[2].wait()
    loads[3].wait()
    heads_per_w = w_rows // HEAD
    for j in range(n_w):
        w_loads[j].wait()
        d = dot(do_in[...], w[pl.ds(j * w_rows, w_rows)], NT).astype(jnp.bfloat16)
        for a in range(heads_per_w):
            h = j * heads_per_w + a
            g, r = h // per, h % per
            for c in range(CHUNKS):
                place = pl.ds(c * crows + r * chunk, chunk)
                dos[g, place] = d[c * chunk : (c + 1) * chunk, a * HEAD : (a + 1) * HEAD]
                qs[g, place] = q_in[pl.ds(c * chunk, chunk), pl.ds(h * HEAD, HEAD)]

    for c in range(CHUNKS):
        first = shard * rows + c * chunk
        q_pos = first + lax.broadcasted_iota(jnp.int32, (chunk, 1), 0)
        start = jnp.zeros((chunk, 1), jnp.int32)
        end = jnp.int32(0)
        for a in range(doc.shape[0]):
            end = end + doc[a]
            start = jnp.maximum(start, jnp.where(end <= q_pos, end, 0))
        k_pos = first - reach_rows + lax.broadcasted_iota(jnp.int32, (chunk, window), 1)
        bias[c] = jnp.where((k_pos >= start) & (k_pos <= q_pos), 0.0, -1e30).astype(jnp.float32)
    if CHUNKS > 1:
        for g in range(groups):
            for c in range(CHUNKS):
                place = pl.ds(c * crows, crows)
                if c > 0:
                    p_ref[g, place, pl.ds(0, c * chunk)] = jnp.zeros((crows, c * chunk), jnp.bfloat16)
                tail = ext - window - c * chunk
                if tail > 0:
                    p_ref[g, place, pl.ds(ext - tail, tail)] = jnp.zeros((crows, tail), jnp.bfloat16)

    def arrive(i):
        @pl.when(shard >= 4)
        def _():
            kv_copy(i, 4).wait_recv()

            @pl.when(jnp.logical_not(even))
            def _():
                fw_copy(i, 4, 3).start()

        @pl.when(shard >= 2)
        def _():
            kv_copy(i, 2).wait_recv()

            @pl.when(even)
            def _():
                fw_copy(i, 2, 3).start()

            @pl.when(jnp.logical_not(even))
            def _():
                fw_copy(i, 2, 1).start()

        @pl.when(shard >= 1)
        def _():
            fw_copy(i, 0, 1).wait_recv()

        @pl.when(shard >= 3)
        def _():
            fw_copy(i, 2, 3).wait_recv()

    order = []
    for a in range((n_t + 1) // 2):
        order.append(n_t - 1 - a)
        if a != n_t - 1 - a:
            order.append(a)

    def cols(d):
        return pl.ds(d * width, width)

    def right_copy(c, d):
        return pltpu.make_async_remote_copy(
            src_ref=part.at[c, d],
            dst_ref=rr.at[c, d],
            send_sem=r_send.at[c, d],
            recv_sem=r_recv.at[c, d],
            device_id={"tensor": t + 1},
            device_id_type=MESH,
        )

    def left_copy(c, d):
        return pltpu.make_async_remote_copy(
            src_ref=part.at[c, d],
            dst_ref=rl.at[c, d],
            send_sem=l_send.at[c, d],
            recv_sem=l_recv.at[c, d],
            device_id={"tensor": t - 1},
            device_id_type=MESH,
        )

    def relay(c, d):
        e = n_t - 1 - d
        if d > 0:

            @pl.when((t > 0) & (t < d))
            def _():
                right_copy(c, d).wait_recv()
                part[c, d] = (part[c, d].astype(jnp.float32) + rr[c, d].astype(jnp.float32)).astype(
                    jnp.bfloat16
                )
                right_copy(c, d).start()

            @pl.when((t < n_t - 1) & (t > e))
            def _():
                left_copy(c, e).wait_recv()
                part[c, e] = (part[c, e].astype(jnp.float32) + rl[c, e].astype(jnp.float32)).astype(
                    jnp.bfloat16
                )
                left_copy(c, e).start()

    factor = scale * math.log2(math.e)
    blocks = crows // ROW_BLOCK
    per_head = chunk // ROW_BLOCK
    arrive(0)
    for c in range(CHUNKS):
        place = pl.ds(c * crows, crows)
        win = pl.ds(c * chunk, window)
        for g in range(groups):
            gc = pl.ds(g * HEAD, HEAD)
            s_ref[...] = dot(qs[g, place], kx[win, gc], NT)

            @pl.loop(0, blocks, unroll=4)
            def _(b):
                row = pl.multiple_of(b * ROW_BLOCK, ROW_BLOCK)
                brow = pl.multiple_of(lax.rem(b, per_head) * ROW_BLOCK, ROW_BLOCK)
                s = s_ref[pl.ds(row, ROW_BLOCK)] + bias[c, pl.ds(brow, ROW_BLOCK)]
                top = jnp.max(s, axis=1, keepdims=True)
                e = jnp.exp2((s - top) * factor)
                inv = 1.0 / jnp.sum(e, axis=1, keepdims=True)
                p_ref[g, pl.ds(c * crows + row, ROW_BLOCK), win] = (e * inv).astype(jnp.bfloat16)

        if c == 0:
            arrive(1)
        for g in range(groups):
            gc = pl.ds(g * HEAD, HEAD)
            o = dot(p_ref[g, place, win], vx[win, gc]).astype(jnp.bfloat16)
            delta[g, place] = jnp.sum(
                o.astype(jnp.float32) * dos[g, place].astype(jnp.float32), axis=1, keepdims=True
            )
            for r in range(per):
                attn[c, :, pl.ds((g * per + r) * HEAD, HEAD)] = o[r * chunk : (r + 1) * chunk]
        for d in order:
            part[c, d] = dot(attn[c], w[:, cols(d)]).astype(jnp.bfloat16)
            if d > 0:

                @pl.when(t == 0)
                def _():
                    right_copy(c, d).start()

            if d < n_t - 1:

                @pl.when(t == n_t - 1)
                def _():
                    left_copy(c, d).start()

    def pair_copy(i, distance):
        src, dst = ((gsk, gpk), (gsv, gpv))[i]
        e = distance // 2
        return pltpu.make_async_remote_copy(
            src_ref=src.at[distance - 1],
            dst_ref=dst.at[e],
            send_sem=p_send.at[i, e],
            recv_sem=p_recv.at[i, e],
            device_id=at_shard(partner),
            device_id_type=MESH,
        )

    def grad_copy(i, distance):
        src, dst = ((gsk, grk), (gsv, grv))[i]
        e = distance // 2 - 1
        return pltpu.make_async_remote_copy(
            src_ref=src.at[distance - 1],
            dst_ref=dst.at[e],
            send_sem=g_send.at[i, e],
            recv_sem=g_recv.at[i, e],
            device_id=at_shard(shard - distance),
            device_id_type=MESH,
        )

    def merge(i, distance, came):
        own, got = ((gsk, gpk), (gsv, gpv))[i]
        pair_copy(i, came).wait_recv()
        own[distance - 1] = (
            own[distance - 1].astype(jnp.float32) + got[came // 2].astype(jnp.float32)
        ).astype(jnp.bfloat16)

    for distance in (3, 1, 4, 2, 0):
        keys = slot(distance)
        for g in range(groups):
            gc = pl.ds(g * HEAD, HEAD)
            dp_ref[...] = dot(dos[g], vx[keys, gc], NT)
            kcols = pl.ds((REACH - distance) * rows, rows)
            ds_ref[...] = (
                p_ref[g, :, kcols].astype(jnp.float32) * (dp_ref[...] - delta[g])
            ).astype(jnp.bfloat16)
            dq = dot(ds_ref[...], kx[keys, gc])
            if distance == 3:
                dq_acc[g] = dq
            else:
                dq_acc[g] += dq
            dk = dot(ds_ref[...], qs[g], TN) * scale
            dv = dot(p_ref[g, :, kcols], dos[g], TN)
            if distance > 0:
                gsk[distance - 1, :, gc] = dk.astype(jnp.bfloat16)
                gsv[distance - 1, :, gc] = dv.astype(jnp.bfloat16)
            else:
                gown[0, :, gc] = dk
                gown[1, :, gc] = dv
        if distance in (1, 3):

            @pl.when(shard >= distance)
            def _():
                for i in range(2):
                    pair_copy(i, distance).start()

        if distance == 4:

            @pl.when(shard >= 4)
            def _():
                for i in range(2):

                    @pl.when(jnp.logical_not(even))
                    def _():
                        merge(i, 4, 3)

                    grad_copy(i, 4).start()

        if distance == 2:

            @pl.when(shard >= 2)
            def _():
                for i in range(2):

                    @pl.when(jnp.logical_not(even))
                    def _():
                        merge(i, 2, 1)

                    @pl.when(even)
                    def _():
                        merge(i, 2, 3)

                    grad_copy(i, 2).start()

            relay(0, n_t - 1)

    @pl.when(even)
    def _():
        for i, ref in enumerate((gpk, gpv)):
            pair_copy(i, 1).wait_recv()
            gown[i] += ref[0].astype(jnp.float32)

    for d in range(n_t - 2, 0, -1):
        relay(0, d)

    for g in range(groups):
        for c in range(CHUNKS):
            for r in range(per):
                gq_ref[pl.ds(c * chunk, chunk), pl.ds((g * per + r) * HEAD, HEAD)] = (
                    dq_acc[g, pl.ds(c * crows + r * chunk, chunk)] * scale
                ).astype(jnp.bfloat16)

    for c in range(1, CHUNKS):
        for d in range(n_t - 1, 0, -1):
            relay(c, d)

    for distance in (4, 2):

        @pl.when(shard + distance < n_shards)
        def _():
            for i, ref in enumerate((grk, grv)):
                grad_copy(i, distance).wait_recv()
                gown[i] += ref[distance // 2 - 1].astype(jnp.float32)

    gk_ref[...] = gown[0].astype(jnp.bfloat16)
    gv_ref[...] = gown[1].astype(jnp.bfloat16)

    for c in range(CHUNKS):
        here = pl.ds(c * chunk, chunk)
        for d in range(n_t):

            @pl.when(t == d)
            def _():
                total = part[c, d].astype(jnp.float32)
                if d > 0:
                    right_copy(c, d).wait_recv()
                    total = total + rr[c, d].astype(jnp.float32)
                if d < n_t - 1:
                    left_copy(c, d).wait_recv()
                    total = total + rl[c, d].astype(jnp.float32)
                out_ref[here] = total.astype(jnp.bfloat16)

    for distance in (4, 2):

        @pl.when(shard + distance < n_shards)
        def _():
            for i in range(2):
                kv_copy(i, distance).wait_send()

    for i in range(2):

        @pl.when(even)
        def _():
            fw_copy(i, 0, 1).wait_send()

        @pl.when(even & (shard >= 2))
        def _():
            fw_copy(i, 2, 3).wait_send()

        @pl.when(jnp.logical_not(even) & (shard >= 2))
        def _():
            fw_copy(i, 2, 1).wait_send()

        @pl.when(jnp.logical_not(even) & (shard >= 4))
        def _():
            fw_copy(i, 4, 3).wait_send()

        for distance in range(1, REACH + 1):

            @pl.when(shard >= distance)
            def _():
                if distance % 2:
                    pair_copy(i, distance).wait_send()
                else:
                    grad_copy(i, distance).wait_send()

    for c in range(CHUNKS):
        for d in range(n_t):

            @pl.when(t < d)
            def _():
                right_copy(c, d).wait_send()

            @pl.when(t > d)
            def _():
                left_copy(c, d).wait_send()


def hand_over(*refs):
    sources, targets, held, in_sem, out_sem = refs[:4], refs[4:8], refs[8:12], refs[12], refs[13]
    ins = [pltpu.make_async_copy(sources[i], held[i], in_sem.at[i]) for i in range(4)]
    outs = [pltpu.make_async_copy(held[i], targets[i], out_sem.at[i]) for i in range(4)]
    for c in ins:
        c.start()
    for i in range(4):
        ins[i].wait()
        outs[i].start()
    for c in outs:
        c.wait()


def shards(sizes, queries, keys, values, doc_lengths, w_out, d_out):
    n_t = sizes[2]
    rows, q_width = queries.shape
    kv_width = keys.shape[1]
    groups = kv_width // HEAD
    heads = q_width // HEAD
    per = heads // groups
    chunk = rows // CHUNKS
    ext = (REACH + 1) * rows
    window = REACH * rows + chunk
    d_model = w_out.shape[1]
    width = d_model // n_t
    bf, f32 = jnp.bfloat16, jnp.float32
    all_rows = per * rows
    n_w = 4
    anywhere = pl.BlockSpec(memory_space=pl.ANY)
    vmem = pl.BlockSpec(memory_space=pltpu.VMEM)
    dma = pltpu.SemaphoreType.DMA
    results = pl.pallas_call(
        functools.partial(kernel, sizes),
        out_shape=(
            jax.ShapeDtypeStruct((rows, width), bf),
            jax.ShapeDtypeStruct((rows, q_width), bf),
            jax.ShapeDtypeStruct((rows, kv_width), bf),
            jax.ShapeDtypeStruct((rows, kv_width), bf),
        ),
        in_specs=[
            anywhere, anywhere, anywhere, pl.BlockSpec(memory_space=pltpu.SMEM), anywhere, anywhere,
        ],
        out_specs=(vmem,) * 4,
        scratch_shapes=[
            pltpu.VMEM((rows, q_width), bf),
            pltpu.VMEM((rows, d_model), bf),
            pltpu.VMEM(w_out.shape, bf),
            pltpu.VMEM((ext, kv_width), bf),
            pltpu.VMEM((ext, kv_width), bf),
            pltpu.VMEM((groups, all_rows, HEAD), bf),
            pltpu.VMEM((groups, all_rows, HEAD), bf),
            pltpu.VMEM((CHUNKS, chunk, q_width), bf),
            pltpu.VMEM((CHUNKS, chunk, window), f32),
            pltpu.VMEM((per * chunk, window), f32),
            pltpu.VMEM((groups, all_rows, ext), bf),
            pltpu.VMEM((groups, all_rows, 1), f32),
            pltpu.VMEM((all_rows, rows), f32),
            pltpu.VMEM((all_rows, rows), bf),
            pltpu.VMEM((groups, all_rows, HEAD), f32),
            pltpu.VMEM((REACH, rows, kv_width), bf),
            pltpu.VMEM((REACH, rows, kv_width), bf),
            pltpu.VMEM((2, rows, kv_width), bf),
            pltpu.VMEM((2, rows, kv_width), bf),
            pltpu.VMEM((2, rows, kv_width), bf),
            pltpu.VMEM((2, rows, kv_width), bf),
            pltpu.VMEM((2, rows, kv_width), f32),
            pltpu.VMEM((CHUNKS, n_t, chunk, width), bf),
            pltpu.VMEM((CHUNKS, n_t, chunk, width), bf),
            pltpu.VMEM((CHUNKS, n_t, chunk, width), bf),
            dma((4,)),
            dma((n_w,)),
            dma((4,)),
            dma((4,)),
            dma((4,)),
            dma((4,)),
            dma((2, 2)),
            dma((2, 2)),
            dma((2, 2)),
            dma((2, 2)),
            dma((CHUNKS, n_t)),
            dma((CHUNKS, n_t)),
            dma((CHUNKS, n_t)),
            dma((CHUNKS, n_t)),
        ],
        compiler_params=pltpu.CompilerParams(
            collective_id=0, has_side_effects=True, vmem_limit_bytes=60 * 1024 * 1024
        ),
        name="layer",
    )(queries, keys, values, doc_lengths, w_out, d_out)
    return pl.pallas_call(
        hand_over,
        out_shape=tuple(jax.ShapeDtypeStruct(x.shape, x.dtype) for x in results),
        in_specs=[anywhere] * 4,
        out_specs=(anywhere,) * 4,
        scratch_shapes=[pltpu.VMEM(x.shape, x.dtype) for x in results] + [dma((4,)), dma((4,))],
        name="hand_over",
    )(*results)


def solution(mesh):
    sizes = tuple(mesh.shape[a] for a in ("seq", "server", "tensor"))
    tokens = P(("seq", "server"), "tensor")
    return jax.shard_map(
        functools.partial(shards, sizes),
        mesh=mesh,
        in_specs=(tokens, tokens, tokens, P(), P("tensor", None), P(("seq", "server"), None)),
        out_specs=(tokens,) * 4,
        check_vma=False,
    )
```

```python
import functools
import math

import jax
import jax.numpy as jnp
from jax import lax
from jax.experimental import pallas as pl
from jax.experimental.pallas import tpu as pltpu
from jax.sharding import PartitionSpec as P

HEAD = 128
REACH = 4
CHUNKS = 2
ROW_BLOCK = 32
MESH = pl.DeviceIdType.MESH
NT = (((1,), (1,)), ((), ()))
TN = (((0,), (0,)), ((), ()))


def dot(a, b, dims=(((1,), (0,)), ((), ()))):
    return lax.dot_general(a, b, dims, preferred_element_type=jnp.float32)


def kernel(
    sizes,
    q_hbm, k_hbm, v_hbm, doc, w_hbm, do_hbm,
    out_ref, gq_ref, gk_ref, gv_ref,
    q_in, do_in, w, kx, vx, qs, dos, attn, bias, s_ref, p_ref, delta,
    dp_ref, ds_ref, dq_acc, gsk, gsv, gpk, gpv, grk, grv, gown, part, rr, rl,
    loc_sem, w_sem, kv_send, kv_recv, fw_send, fw_recv, p_send, p_recv, g_send, g_recv,
    r_send, r_recv, l_send, l_recv,
):
    n_seq, n_server, n_t = sizes
    n_shards = n_seq * n_server
    rows = q_in.shape[0]
    heads = q_in.shape[1] // HEAD
    groups = kx.shape[1] // HEAD
    per = heads // groups
    chunk = rows // CHUNKS
    ext = kx.shape[0]
    reach_rows = REACH * rows
    window = reach_rows + chunk
    crows = per * chunk
    width = out_ref.shape[1]
    scale = HEAD ** -0.5

    shard = lax.axis_index("seq") * n_server + lax.axis_index("server")
    t = lax.axis_index("tensor")

    def at_shard(other):
        return {"seq": other // n_server, "server": lax.rem(other, n_server)}

    loads = [
        pltpu.make_async_copy(k_hbm, kx.at[pl.ds(reach_rows, rows)], loc_sem.at[0]),
        pltpu.make_async_copy(v_hbm, vx.at[pl.ds(reach_rows, rows)], loc_sem.at[1]),
        pltpu.make_async_copy(do_hbm, do_in, loc_sem.at[2]),
        pltpu.make_async_copy(q_hbm, q_in, loc_sem.at[3]),
    ]
    n_w = w_sem.shape[0]
    w_rows = w.shape[0] // n_w
    w_loads = [
        pltpu.make_async_copy(
            w_hbm.at[pl.ds(j * w_rows, w_rows)], w.at[pl.ds(j * w_rows, w_rows)], w_sem.at[j]
        )
        for j in range(n_w)
    ]
    for c in loads:
        c.start()
    for c in w_loads:
        c.start()

    barrier = pltpu.get_barrier_semaphore()
    count = jnp.int32(0)
    partner = shard + 1 - 2 * lax.rem(shard, 2)
    pl.semaphore_signal(barrier, inc=1, device_id=at_shard(partner), device_id_type=MESH)
    count = count + 1
    for step in (2, 4):
        for sign in (1, -1):
            other = shard + sign * step
            ok = (other >= 0) & (other < n_shards)

            @pl.when(ok)
            def _():
                pl.semaphore_signal(barrier, inc=1, device_id=at_shard(other), device_id_type=MESH)

            count = count + ok.astype(jnp.int32)
    for sign in (1, -1):
        other = t + sign
        ok = (other >= 0) & (other < n_t)

        @pl.when(ok)
        def _():
            pl.semaphore_signal(barrier, inc=1, device_id={"tensor": other}, device_id_type=MESH)

        count = count + ok.astype(jnp.int32)
    pl.semaphore_wait(barrier, count)

    def slot(distance):
        return pl.ds((REACH - distance) * rows, rows)

    def kv_copy(i, distance):
        src, dst = ((k_hbm, kx), (v_hbm, vx))[i]
        e = 2 * (distance // 2 - 1) + i
        return pltpu.make_async_remote_copy(
            src_ref=src,
            dst_ref=dst.at[slot(distance)],
            send_sem=kv_send.at[e],
            recv_sem=kv_recv.at[e],
            device_id=at_shard(shard + distance),
            device_id_type=MESH,
        )

    even = lax.rem(shard, 2) == 0

    def fw_copy(i, from_distance, to_distance):
        ref = (kx, vx)[i]
        e = 2 * (to_distance // 2) + i
        return pltpu.make_async_remote_copy(
            src_ref=ref.at[slot(from_distance)],
            dst_ref=ref.at[slot(to_distance)],
            send_sem=fw_send.at[e],
            recv_sem=fw_recv.at[e],
            device_id=at_shard(partner),
            device_id_type=MESH,
        )

    for i in range(2):
        for distance in (4, 2):

            @pl.when(shard + distance < n_shards)
            def _():
                kv_copy(i, distance).start()

    for c in loads[:2]:
        c.wait()

    @pl.when(even)
    def _():
        for i in range(2):
            fw_copy(i, 0, 1).start()

    for distance in range(1, REACH + 1):

        @pl.when(shard < distance)
        def _():
            kx[slot(distance)] = jnp.zeros((rows, kx.shape[1]), kx.dtype)
            vx[slot(distance)] = jnp.zeros((rows, kx.shape[1]), kx.dtype)

    loads[2].wait()
    loads[3].wait()
    heads_per_w = w_rows // HEAD
    for j in range(n_w):
        w_loads[j].wait()
        d = dot(do_in[...], w[pl.ds(j * w_rows, w_rows)], NT).astype(jnp.bfloat16)
        for a in range(heads_per_w):
            h = j * heads_per_w + a
            g, r = h // per, h % per
            for c in range(CHUNKS):
                place = pl.ds(c * crows + r * chunk, chunk)
                dos[g, place] = d[c * chunk : (c + 1) * chunk, a * HEAD : (a + 1) * HEAD]
                qs[g, place] = q_in[pl.ds(c * chunk, chunk), pl.ds(h * HEAD, HEAD)]

    for c in range(CHUNKS):
        first = shard * rows + c * chunk
        q_pos = first + lax.broadcasted_iota(jnp.int32, (chunk, 1), 0)
        start = jnp.zeros((chunk, 1), jnp.int32)
        end = jnp.int32(0)
        for a in range(doc.shape[0]):
            end = end + doc[a]
            start = jnp.maximum(start, jnp.where(end <= q_pos, end, 0))
        k_pos = first - reach_rows + lax.broadcasted_iota(jnp.int32, (chunk, window), 1)
        bias[c] = jnp.where((k_pos >= start) & (k_pos <= q_pos), 0.0, -1e30).astype(jnp.float32)
    if CHUNKS > 1:
        for g in range(groups):
            for c in range(CHUNKS):
                place = pl.ds(c * crows, crows)
                if c > 0:
                    p_ref[g, place, pl.ds(0, c * chunk)] = jnp.zeros((crows, c * chunk), jnp.bfloat16)
                tail = ext - window - c * chunk
                if tail > 0:
                    p_ref[g, place, pl.ds(ext - tail, tail)] = jnp.zeros((crows, tail), jnp.bfloat16)

    def arrive(i):
        @pl.when(shard >= 4)
        def _():
            kv_copy(i, 4).wait_recv()

            @pl.when(jnp.logical_not(even))
            def _():
                fw_copy(i, 4, 3).start()

        @pl.when(shard >= 2)
        def _():
            kv_copy(i, 2).wait_recv()

            @pl.when(even)
            def _():
                fw_copy(i, 2, 3).start()

            @pl.when(jnp.logical_not(even))
            def _():
                fw_copy(i, 2, 1).start()

        @pl.when(shard >= 1)
        def _():
            fw_copy(i, 0, 1).wait_recv()

        @pl.when(shard >= 3)
        def _():
            fw_copy(i, 2, 3).wait_recv()

    order = []
    for a in range((n_t + 1) // 2):
        order.append(n_t - 1 - a)
        if a != n_t - 1 - a:
            order.append(a)

    def cols(d):
        return pl.ds(d * width, width)

    def right_copy(c, d):
        return pltpu.make_async_remote_copy(
            src_ref=part.at[c, d],
            dst_ref=rr.at[c, d],
            send_sem=r_send.at[c, d],
            recv_sem=r_recv.at[c, d],
            device_id={"tensor": t + 1},
            device_id_type=MESH,
        )

    def left_copy(c, d):
        return pltpu.make_async_remote_copy(
            src_ref=part.at[c, d],
            dst_ref=rl.at[c, d],
            send_sem=l_send.at[c, d],
            recv_sem=l_recv.at[c, d],
            device_id={"tensor": t - 1},
            device_id_type=MESH,
        )

    def pass_on(copy, came, c, d):
        copy(c, d).wait_recv()
        part[c, d] = (part[c, d].astype(jnp.float32) + came[c, d].astype(jnp.float32)).astype(
            jnp.bfloat16
        )
        copy(c, d).start()

    def relay(c, step):
        for here in range(1, n_t - 1):
            right = [(k + here, 0, n_t - 1 - k) for k in range(n_t - 1 - here)]
            left = [(k + n_t - 1 - here, 1, k) for k in range(here)]
            due = [x for x in sorted(right + left) if x[0] == step]
            if 2 * here >= n_t:
                due = due[::-1]
            if due:

                @pl.when(t == here)
                def _():
                    for _, way, d in due:
                        if way == 0:
                            pass_on(right_copy, rr, c, d)
                        else:
                            pass_on(left_copy, rl, c, d)

    factor = scale * math.log2(math.e)
    blocks = crows // ROW_BLOCK
    per_head = chunk // ROW_BLOCK
    arrive(0)
    for c in range(CHUNKS):
        place = pl.ds(c * crows, crows)
        win = pl.ds(c * chunk, window)
        for g in range(groups):
            gc = pl.ds(g * HEAD, HEAD)
            s_ref[...] = dot(qs[g, place], kx[win, gc], NT)

            @pl.loop(0, blocks, unroll=4)
            def _(b):
                row = pl.multiple_of(b * ROW_BLOCK, ROW_BLOCK)
                brow = pl.multiple_of(lax.rem(b, per_head) * ROW_BLOCK, ROW_BLOCK)
                s = s_ref[pl.ds(row, ROW_BLOCK)] + bias[c, pl.ds(brow, ROW_BLOCK)]
                top = jnp.max(s, axis=1, keepdims=True)
                e = jnp.exp2((s - top) * factor)
                inv = 1.0 / jnp.sum(e, axis=1, keepdims=True)
                p_ref[g, pl.ds(c * crows + row, ROW_BLOCK), win] = (e * inv).astype(jnp.bfloat16)

        if c == 0:
            arrive(1)
        for g in range(groups):
            gc = pl.ds(g * HEAD, HEAD)
            o = dot(p_ref[g, place, win], vx[win, gc]).astype(jnp.bfloat16)
            delta[g, place] = jnp.sum(
                o.astype(jnp.float32) * dos[g, place].astype(jnp.float32), axis=1, keepdims=True
            )
            for r in range(per):
                attn[c, :, pl.ds((g * per + r) * HEAD, HEAD)] = o[r * chunk : (r + 1) * chunk]
        done, right_next, left_next = [], n_t - 1, 0
        for d in order:
            part[c, d] = dot(attn[c], w[:, cols(d)]).astype(jnp.bfloat16)
            done.append(d)
            while right_next > 0 and right_next in done:
                d_right = right_next

                @pl.when(t == 0)
                def _():
                    right_copy(c, d_right).start()

                right_next -= 1
            while left_next < n_t - 1 and left_next in done:
                d_left = left_next

                @pl.when(t == n_t - 1)
                def _():
                    left_copy(c, d_left).start()

                left_next += 1

    def pair_copy(i, distance):
        src, dst = ((gsk, gpk), (gsv, gpv))[i]
        e = distance // 2
        return pltpu.make_async_remote_copy(
            src_ref=src.at[distance - 1],
            dst_ref=dst.at[e],
            send_sem=p_send.at[i, e],
            recv_sem=p_recv.at[i, e],
            device_id=at_shard(partner),
            device_id_type=MESH,
        )

    def grad_copy(i, distance):
        src, dst = ((gsk, grk), (gsv, grv))[i]
        e = distance // 2 - 1
        return pltpu.make_async_remote_copy(
            src_ref=src.at[distance - 1],
            dst_ref=dst.at[e],
            send_sem=g_send.at[i, e],
            recv_sem=g_recv.at[i, e],
            device_id=at_shard(shard - distance),
            device_id_type=MESH,
        )

    def merge(i, distance, came):
        own, got = ((gsk, gpk), (gsv, gpv))[i]
        pair_copy(i, came).wait_recv()
        own[distance - 1] = (
            own[distance - 1].astype(jnp.float32) + got[came // 2].astype(jnp.float32)
        ).astype(jnp.bfloat16)

    relay(0, 1)
    for distance in (3, 1, 4, 2, 0):
        if distance == 2:
            relay(0, 2)
        keys = slot(distance)
        for g in range(groups):
            gc = pl.ds(g * HEAD, HEAD)
            dp_ref[...] = dot(dos[g], vx[keys, gc], NT)
            kcols = pl.ds((REACH - distance) * rows, rows)
            ds_ref[...] = (
                p_ref[g, :, kcols].astype(jnp.float32) * (dp_ref[...] - delta[g])
            ).astype(jnp.bfloat16)
            dq = dot(ds_ref[...], kx[keys, gc])
            if distance == 3:
                dq_acc[g] = dq
            else:
                dq_acc[g] += dq
            dk = dot(ds_ref[...], qs[g], TN) * scale
            dv = dot(p_ref[g, :, kcols], dos[g], TN)
            if distance > 0:
                gsk[distance - 1, :, gc] = dk.astype(jnp.bfloat16)
                gsv[distance - 1, :, gc] = dv.astype(jnp.bfloat16)
            else:
                gown[0, :, gc] = dk
                gown[1, :, gc] = dv
        if distance in (1, 3):

            @pl.when(shard >= distance)
            def _():
                for i in range(2):
                    pair_copy(i, distance).start()

        if distance == 4:

            @pl.when(shard >= 4)
            def _():
                for i in range(2):

                    @pl.when(jnp.logical_not(even))
                    def _():
                        merge(i, 4, 3)

                    grad_copy(i, 4).start()

        if distance == 2:

            @pl.when(shard >= 2)
            def _():
                for i in range(2):

                    @pl.when(jnp.logical_not(even))
                    def _():
                        merge(i, 2, 1)

                    @pl.when(even)
                    def _():
                        merge(i, 2, 3)

                    grad_copy(i, 2).start()

    @pl.when(even)
    def _():
        for i, ref in enumerate((gpk, gpv)):
            pair_copy(i, 1).wait_recv()
            gown[i] += ref[0].astype(jnp.float32)

    for step in range(3, n_t - 1):
        relay(0, step)

    for g in range(groups):
        for c in range(CHUNKS):
            for r in range(per):
                gq_ref[pl.ds(c * chunk, chunk), pl.ds((g * per + r) * HEAD, HEAD)] = (
                    dq_acc[g, pl.ds(c * crows + r * chunk, chunk)] * scale
                ).astype(jnp.bfloat16)

    for c in range(1, CHUNKS):
        for step in range(1, n_t - 1):
            relay(c, step)

    for distance in (4, 2):

        @pl.when(shard + distance < n_shards)
        def _():
            for i, ref in enumerate((grk, grv)):
                grad_copy(i, distance).wait_recv()
                gown[i] += ref[distance // 2 - 1].astype(jnp.float32)

    gk_ref[...] = gown[0].astype(jnp.bfloat16)
    gv_ref[...] = gown[1].astype(jnp.bfloat16)

    for c in range(CHUNKS):
        here = pl.ds(c * chunk, chunk)
        for d in range(n_t):

            @pl.when(t == d)
            def _():
                total = part[c, d].astype(jnp.float32)
                if d > 0:
                    right_copy(c, d).wait_recv()
                    total = total + rr[c, d].astype(jnp.float32)
                if d < n_t - 1:
                    left_copy(c, d).wait_recv()
                    total = total + rl[c, d].astype(jnp.float32)
                out_ref[here] = total.astype(jnp.bfloat16)

    for distance in (4, 2):

        @pl.when(shard + distance < n_shards)
        def _():
            for i in range(2):
                kv_copy(i, distance).wait_send()

    for i in range(2):

        @pl.when(even)
        def _():
            fw_copy(i, 0, 1).wait_send()

        @pl.when(even & (shard >= 2))
        def _():
            fw_copy(i, 2, 3).wait_send()

        @pl.when(jnp.logical_not(even) & (shard >= 2))
        def _():
            fw_copy(i, 2, 1).wait_send()

        @pl.when(jnp.logical_not(even) & (shard >= 4))
        def _():
            fw_copy(i, 4, 3).wait_send()

        for distance in range(1, REACH + 1):

            @pl.when(shard >= distance)
            def _():
                if distance % 2:
                    pair_copy(i, distance).wait_send()
                else:
                    grad_copy(i, distance).wait_send()

    for c in range(CHUNKS):
        for d in range(n_t):

            @pl.when(t < d)
            def _():
                right_copy(c, d).wait_send()

            @pl.when(t > d)
            def _():
                left_copy(c, d).wait_send()


def hand_over(*refs):
    sources, targets, held, in_sem, out_sem = refs[:4], refs[4:8], refs[8:12], refs[12], refs[13]
    ins = [pltpu.make_async_copy(sources[i], held[i], in_sem.at[i]) for i in range(4)]
    outs = [pltpu.make_async_copy(held[i], targets[i], out_sem.at[i]) for i in range(4)]
    for c in ins:
        c.start()
    for i in range(4):
        ins[i].wait()
        outs[i].start()
    for c in outs:
        c.wait()


def shards(sizes, queries, keys, values, doc_lengths, w_out, d_out):
    n_t = sizes[2]
    rows, q_width = queries.shape
    kv_width = keys.shape[1]
    groups = kv_width // HEAD
    heads = q_width // HEAD
    per = heads // groups
    chunk = rows // CHUNKS
    ext = (REACH + 1) * rows
    window = REACH * rows + chunk
    d_model = w_out.shape[1]
    width = d_model // n_t
    bf, f32 = jnp.bfloat16, jnp.float32
    all_rows = per * rows
    n_w = 4
    anywhere = pl.BlockSpec(memory_space=pl.ANY)
    vmem = pl.BlockSpec(memory_space=pltpu.VMEM)
    dma = pltpu.SemaphoreType.DMA
    results = pl.pallas_call(
        functools.partial(kernel, sizes),
        out_shape=(
            jax.ShapeDtypeStruct((rows, width), bf),
            jax.ShapeDtypeStruct((rows, q_width), bf),
            jax.ShapeDtypeStruct((rows, kv_width), bf),
            jax.ShapeDtypeStruct((rows, kv_width), bf),
        ),
        in_specs=[
            anywhere, anywhere, anywhere, pl.BlockSpec(memory_space=pltpu.SMEM), anywhere, anywhere,
        ],
        out_specs=(vmem,) * 4,
        scratch_shapes=[
            pltpu.VMEM((rows, q_width), bf),
            pltpu.VMEM((rows, d_model), bf),
            pltpu.VMEM(w_out.shape, bf),
            pltpu.VMEM((ext, kv_width), bf),
            pltpu.VMEM((ext, kv_width), bf),
            pltpu.VMEM((groups, all_rows, HEAD), bf),
            pltpu.VMEM((groups, all_rows, HEAD), bf),
            pltpu.VMEM((CHUNKS, chunk, q_width), bf),
            pltpu.VMEM((CHUNKS, chunk, window), f32),
            pltpu.VMEM((per * chunk, window), f32),
            pltpu.VMEM((groups, all_rows, ext), bf),
            pltpu.VMEM((groups, all_rows, 1), f32),
            pltpu.VMEM((all_rows, rows), f32),
            pltpu.VMEM((all_rows, rows), bf),
            pltpu.VMEM((groups, all_rows, HEAD), f32),
            pltpu.VMEM((REACH, rows, kv_width), bf),
            pltpu.VMEM((REACH, rows, kv_width), bf),
            pltpu.VMEM((2, rows, kv_width), bf),
            pltpu.VMEM((2, rows, kv_width), bf),
            pltpu.VMEM((2, rows, kv_width), bf),
            pltpu.VMEM((2, rows, kv_width), bf),
            pltpu.VMEM((2, rows, kv_width), f32),
            pltpu.VMEM((CHUNKS, n_t, chunk, width), bf),
            pltpu.VMEM((CHUNKS, n_t, chunk, width), bf),
            pltpu.VMEM((CHUNKS, n_t, chunk, width), bf),
            dma((4,)),
            dma((n_w,)),
            dma((4,)),
            dma((4,)),
            dma((4,)),
            dma((4,)),
            dma((2, 2)),
            dma((2, 2)),
            dma((2, 2)),
            dma((2, 2)),
            dma((CHUNKS, n_t)),
            dma((CHUNKS, n_t)),
            dma((CHUNKS, n_t)),
            dma((CHUNKS, n_t)),
        ],
        compiler_params=pltpu.CompilerParams(
            collective_id=0, has_side_effects=True, vmem_limit_bytes=60 * 1024 * 1024
        ),
        name="layer",
    )(queries, keys, values, doc_lengths, w_out, d_out)
    return pl.pallas_call(
        hand_over,
        out_shape=tuple(jax.ShapeDtypeStruct(x.shape, x.dtype) for x in results),
        in_specs=[anywhere] * 4,
        out_specs=(anywhere,) * 4,
        scratch_shapes=[pltpu.VMEM(x.shape, x.dtype) for x in results] + [dma((4,)), dma((4,))],
        name="hand_over",
    )(*results)


def solution(mesh):
    sizes = tuple(mesh.shape[a] for a in ("seq", "server", "tensor"))
    tokens = P(("seq", "server"), "tensor")
    return jax.shard_map(
        functools.partial(shards, sizes),
        mesh=mesh,
        in_specs=(tokens, tokens, tokens, P(), P("tensor", None), P(("seq", "server"), None)),
        out_specs=(tokens,) * 4,
        check_vma=False,
    )
```

```python
import functools
import math

import jax
import jax.numpy as jnp
from jax import lax
from jax.experimental import pallas as pl
from jax.experimental.pallas import tpu as pltpu
from jax.sharding import PartitionSpec as P

HEAD = 128
REACH = 4
CHUNKS = 2
ROW_BLOCK = 32
MESH = pl.DeviceIdType.MESH
NT = (((1,), (1,)), ((), ()))
TN = (((0,), (0,)), ((), ()))


def dot(a, b, dims=(((1,), (0,)), ((), ()))):
    return lax.dot_general(a, b, dims, preferred_element_type=jnp.float32)


def kernel(
    sizes,
    q_hbm, k_hbm, v_hbm, doc, w_hbm, do_hbm,
    out_ref, gq_ref, gk_ref, gv_ref,
    q_in, do_in, w, kx, vx, qs, dos, attn, bias, s_ref, p_ref, delta,
    dp_ref, ds_ref, dq_acc, gsk, gsv, gpk, gpv, grk, grv, gown, part, rr, rl,
    loc_sem, w_sem, kv_send, kv_recv, fw_send, fw_recv, p_send, p_recv, g_send, g_recv,
    r_send, r_recv, l_send, l_recv,
):
    n_seq, n_server, n_t = sizes
    n_shards = n_seq * n_server
    rows = q_in.shape[0]
    heads = q_in.shape[1] // HEAD
    groups = kx.shape[1] // HEAD
    per = heads // groups
    chunk = rows // CHUNKS
    ext = kx.shape[0]
    reach_rows = REACH * rows
    window = reach_rows + chunk
    crows = per * chunk
    width = out_ref.shape[1]
    scale = HEAD ** -0.5

    shard = lax.axis_index("seq") * n_server + lax.axis_index("server")
    t = lax.axis_index("tensor")

    def at_shard(other):
        return {"seq": other // n_server, "server": lax.rem(other, n_server)}

    loads = [
        pltpu.make_async_copy(k_hbm, kx.at[pl.ds(reach_rows, rows)], loc_sem.at[0]),
        pltpu.make_async_copy(v_hbm, vx.at[pl.ds(reach_rows, rows)], loc_sem.at[1]),
        pltpu.make_async_copy(do_hbm, do_in, loc_sem.at[2]),
        pltpu.make_async_copy(q_hbm, q_in, loc_sem.at[3]),
    ]
    n_w = w_sem.shape[0]
    w_rows = w.shape[0] // n_w
    w_loads = [
        pltpu.make_async_copy(
            w_hbm.at[pl.ds(j * w_rows, w_rows)], w.at[pl.ds(j * w_rows, w_rows)], w_sem.at[j]
        )
        for j in range(n_w)
    ]
    for c in loads:
        c.start()
    for c in w_loads:
        c.start()

    barrier = pltpu.get_barrier_semaphore()
    count = jnp.int32(0)
    partner = shard + 1 - 2 * lax.rem(shard, 2)
    pl.semaphore_signal(barrier, inc=1, device_id=at_shard(partner), device_id_type=MESH)
    count = count + 1
    for step in (2, 4):
        for sign in (1, -1):
            other = shard + sign * step
            ok = (other >= 0) & (other < n_shards)

            @pl.when(ok)
            def _():
                pl.semaphore_signal(barrier, inc=1, device_id=at_shard(other), device_id_type=MESH)

            count = count + ok.astype(jnp.int32)
    for sign in (1, -1):
        other = t + sign
        ok = (other >= 0) & (other < n_t)

        @pl.when(ok)
        def _():
            pl.semaphore_signal(barrier, inc=1, device_id={"tensor": other}, device_id_type=MESH)

        count = count + ok.astype(jnp.int32)
    pl.semaphore_wait(barrier, count)

    def slot(distance):
        return pl.ds((REACH - distance) * rows, rows)

    def kv_copy(i, distance):
        src, dst = ((k_hbm, kx), (v_hbm, vx))[i]
        e = 2 * (distance // 2 - 1) + i
        return pltpu.make_async_remote_copy(
            src_ref=src,
            dst_ref=dst.at[slot(distance)],
            send_sem=kv_send.at[e],
            recv_sem=kv_recv.at[e],
            device_id=at_shard(shard + distance),
            device_id_type=MESH,
        )

    even = lax.rem(shard, 2) == 0

    def fw_copy(i, from_distance, to_distance):
        ref = (kx, vx)[i]
        e = 2 * (to_distance // 2) + i
        return pltpu.make_async_remote_copy(
            src_ref=ref.at[slot(from_distance)],
            dst_ref=ref.at[slot(to_distance)],
            send_sem=fw_send.at[e],
            recv_sem=fw_recv.at[e],
            device_id=at_shard(partner),
            device_id_type=MESH,
        )

    for i in range(2):
        for distance in (4, 2):

            @pl.when(shard + distance < n_shards)
            def _():
                kv_copy(i, distance).start()

    for c in loads[:2]:
        c.wait()

    @pl.when(even)
    def _():
        for i in range(2):
            fw_copy(i, 0, 1).start()

    for distance in range(1, REACH + 1):

        @pl.when(shard < distance)
        def _():
            kx[slot(distance)] = jnp.zeros((rows, kx.shape[1]), kx.dtype)
            vx[slot(distance)] = jnp.zeros((rows, kx.shape[1]), kx.dtype)

    loads[2].wait()
    loads[3].wait()
    heads_per_w = w_rows // HEAD
    for j in range(n_w):
        w_loads[j].wait()
        d = dot(do_in[...], w[pl.ds(j * w_rows, w_rows)], NT).astype(jnp.bfloat16)
        for a in range(heads_per_w):
            h = j * heads_per_w + a
            g, r = h // per, h % per
            for c in range(CHUNKS):
                place = pl.ds(c * crows + r * chunk, chunk)
                dos[g, place] = d[c * chunk : (c + 1) * chunk, a * HEAD : (a + 1) * HEAD]
                qs[g, place] = q_in[pl.ds(c * chunk, chunk), pl.ds(h * HEAD, HEAD)]

    def arrive(i):
        @pl.when(shard >= 4)
        def _():
            kv_copy(i, 4).wait_recv()

            @pl.when(jnp.logical_not(even))
            def _():
                fw_copy(i, 4, 3).start()

        @pl.when(shard >= 2)
        def _():
            kv_copy(i, 2).wait_recv()

            @pl.when(even)
            def _():
                fw_copy(i, 2, 3).start()

            @pl.when(jnp.logical_not(even))
            def _():
                fw_copy(i, 2, 1).start()

    def arrived(i):
        @pl.when(shard >= 1)
        def _():
            fw_copy(i, 0, 1).wait_recv()

        @pl.when(shard >= 3)
        def _():
            fw_copy(i, 2, 3).wait_recv()

    arrive(0)

    for c in range(CHUNKS):
        first = shard * rows + c * chunk
        q_pos = first + lax.broadcasted_iota(jnp.int32, (chunk, 1), 0)
        start = jnp.zeros((chunk, 1), jnp.int32)
        end = jnp.int32(0)
        for a in range(doc.shape[0]):
            end = end + doc[a]
            start = jnp.maximum(start, jnp.where(end <= q_pos, end, 0))
        k_pos = first - reach_rows + lax.broadcasted_iota(jnp.int32, (chunk, window), 1)
        bias[c] = jnp.where((k_pos >= start) & (k_pos <= q_pos), 0.0, -1e30).astype(jnp.float32)
    if CHUNKS > 1:
        for g in range(groups):
            for c in range(CHUNKS):
                place = pl.ds(c * crows, crows)
                if c > 0:
                    p_ref[g, place, pl.ds(0, c * chunk)] = jnp.zeros((crows, c * chunk), jnp.bfloat16)
                tail = ext - window - c * chunk
                if tail > 0:
                    p_ref[g, place, pl.ds(ext - tail, tail)] = jnp.zeros((crows, tail), jnp.bfloat16)

    order = []
    for a in range((n_t + 1) // 2):
        order.append(n_t - 1 - a)
        if a != n_t - 1 - a:
            order.append(a)

    def cols(d):
        return pl.ds(d * width, width)

    def right_copy(c, d):
        return pltpu.make_async_remote_copy(
            src_ref=part.at[c, d],
            dst_ref=rr.at[c, d],
            send_sem=r_send.at[c, d],
            recv_sem=r_recv.at[c, d],
            device_id={"tensor": t + 1},
            device_id_type=MESH,
        )

    def left_copy(c, d):
        return pltpu.make_async_remote_copy(
            src_ref=part.at[c, d],
            dst_ref=rl.at[c, d],
            send_sem=l_send.at[c, d],
            recv_sem=l_recv.at[c, d],
            device_id={"tensor": t - 1},
            device_id_type=MESH,
        )

    def pass_on(copy, came, c, d):
        copy(c, d).wait_recv()
        part[c, d] = (part[c, d].astype(jnp.float32) + came[c, d].astype(jnp.float32)).astype(
            jnp.bfloat16
        )
        copy(c, d).start()

    def relay(c, step):
        for here in range(1, n_t - 1):
            right = [(k + here, 0, n_t - 1 - k) for k in range(n_t - 1 - here)]
            left = [(k + n_t - 1 - here, 1, k) for k in range(here)]
            due = [x for x in sorted(right + left) if x[0] == step]
            if 2 * here >= n_t:
                due = due[::-1]
            if due:

                @pl.when(t == here)
                def _():
                    for _, way, d in due:
                        if way == 0:
                            pass_on(right_copy, rr, c, d)
                        else:
                            pass_on(left_copy, rl, c, d)

    factor = scale * math.log2(math.e)
    blocks = crows // ROW_BLOCK
    per_head = chunk // ROW_BLOCK
    arrived(0)
    for c in range(CHUNKS):
        place = pl.ds(c * crows, crows)
        win = pl.ds(c * chunk, window)
        for g in range(groups):
            gc = pl.ds(g * HEAD, HEAD)
            s_ref[...] = dot(qs[g, place], kx[win, gc], NT)

            @pl.loop(0, blocks, unroll=4)
            def _(b):
                row = pl.multiple_of(b * ROW_BLOCK, ROW_BLOCK)
                brow = pl.multiple_of(lax.rem(b, per_head) * ROW_BLOCK, ROW_BLOCK)
                s = s_ref[pl.ds(row, ROW_BLOCK)] + bias[c, pl.ds(brow, ROW_BLOCK)]
                top = jnp.max(s, axis=1, keepdims=True)
                e = jnp.exp2((s - top) * factor)
                inv = 1.0 / jnp.sum(e, axis=1, keepdims=True)
                p_ref[g, pl.ds(c * crows + row, ROW_BLOCK), win] = (e * inv).astype(jnp.bfloat16)

            if c == 0 and g == 0:
                arrive(1)

        if c == 0:
            arrived(1)
        for g in range(groups):
            gc = pl.ds(g * HEAD, HEAD)
            o = dot(p_ref[g, place, win], vx[win, gc]).astype(jnp.bfloat16)
            delta[g, place] = jnp.sum(
                o.astype(jnp.float32) * dos[g, place].astype(jnp.float32), axis=1, keepdims=True
            )
            for r in range(per):
                attn[c, :, pl.ds((g * per + r) * HEAD, HEAD)] = o[r * chunk : (r + 1) * chunk]
        done, right_next, left_next = [], n_t - 1, 0
        for d in order:
            part[c, d] = dot(attn[c], w[:, cols(d)]).astype(jnp.bfloat16)
            done.append(d)
            while right_next > 0 and right_next in done:
                d_right = right_next

                @pl.when(t == 0)
                def _():
                    right_copy(c, d_right).start()

                right_next -= 1
            while left_next < n_t - 1 and left_next in done:
                d_left = left_next

                @pl.when(t == n_t - 1)
                def _():
                    left_copy(c, d_left).start()

                left_next += 1

    def pair_copy(i, distance):
        src, dst = ((gsk, gpk), (gsv, gpv))[i]
        e = distance // 2
        return pltpu.make_async_remote_copy(
            src_ref=src.at[distance - 1],
            dst_ref=dst.at[e],
            send_sem=p_send.at[i, e],
            recv_sem=p_recv.at[i, e],
            device_id=at_shard(partner),
            device_id_type=MESH,
        )

    def grad_copy(i, distance):
        src, dst = ((gsk, grk), (gsv, grv))[i]
        e = distance // 2 - 1
        return pltpu.make_async_remote_copy(
            src_ref=src.at[distance - 1],
            dst_ref=dst.at[e],
            send_sem=g_send.at[i, e],
            recv_sem=g_recv.at[i, e],
            device_id=at_shard(shard - distance),
            device_id_type=MESH,
        )

    def merge(i, distance, came):
        own, got = ((gsk, gpk), (gsv, gpv))[i]
        pair_copy(i, came).wait_recv()
        own[distance - 1] = (
            own[distance - 1].astype(jnp.float32) + got[came // 2].astype(jnp.float32)
        ).astype(jnp.bfloat16)

    relay(0, 1)
    for distance in (3, 1, 4, 2, 0):
        if distance == 2:
            relay(0, 2)
        keys = slot(distance)
        for g in range(groups):
            gc = pl.ds(g * HEAD, HEAD)
            dp_ref[...] = dot(dos[g], vx[keys, gc], NT)
            kcols = pl.ds((REACH - distance) * rows, rows)
            ds_ref[...] = (
                p_ref[g, :, kcols].astype(jnp.float32) * (dp_ref[...] - delta[g])
            ).astype(jnp.bfloat16)
            dq = dot(ds_ref[...], kx[keys, gc])
            if distance == 3:
                dq_acc[g] = dq
            else:
                dq_acc[g] += dq
            dk = dot(ds_ref[...], qs[g], TN) * scale
            dv = dot(p_ref[g, :, kcols], dos[g], TN)
            if distance > 0:
                gsk[distance - 1, :, gc] = dk.astype(jnp.bfloat16)
                gsv[distance - 1, :, gc] = dv.astype(jnp.bfloat16)
            else:
                gown[0, :, gc] = dk
                gown[1, :, gc] = dv
        if distance in (1, 3):

            @pl.when(shard >= distance)
            def _():
                for i in range(2):
                    pair_copy(i, distance).start()

        if distance == 4:

            @pl.when(shard >= 4)
            def _():
                for i in range(2):

                    @pl.when(jnp.logical_not(even))
                    def _():
                        merge(i, 4, 3)

                    grad_copy(i, 4).start()

        if distance == 2:

            @pl.when(shard >= 2)
            def _():
                for i in range(2):

                    @pl.when(jnp.logical_not(even))
                    def _():
                        merge(i, 2, 1)

                    @pl.when(even)
                    def _():
                        merge(i, 2, 3)

                    grad_copy(i, 2).start()

    @pl.when(even)
    def _():
        for i, ref in enumerate((gpk, gpv)):
            pair_copy(i, 1).wait_recv()
            gown[i] += ref[0].astype(jnp.float32)

    for step in range(3, n_t - 1):
        relay(0, step)

    for g in range(groups):
        for c in range(CHUNKS):
            for r in range(per):
                gq_ref[pl.ds(c * chunk, chunk), pl.ds((g * per + r) * HEAD, HEAD)] = (
                    dq_acc[g, pl.ds(c * crows + r * chunk, chunk)] * scale
                ).astype(jnp.bfloat16)

    for c in range(1, CHUNKS):
        for step in range(1, n_t - 1):
            relay(c, step)

    for distance in (4, 2):

        @pl.when(shard + distance < n_shards)
        def _():
            for i, ref in enumerate((grk, grv)):
                grad_copy(i, distance).wait_recv()
                gown[i] += ref[distance // 2 - 1].astype(jnp.float32)

    gk_ref[...] = gown[0].astype(jnp.bfloat16)
    gv_ref[...] = gown[1].astype(jnp.bfloat16)

    for c in range(CHUNKS):
        here = pl.ds(c * chunk, chunk)
        for d in range(n_t):

            @pl.when(t == d)
            def _():
                total = part[c, d].astype(jnp.float32)
                if d > 0:
                    right_copy(c, d).wait_recv()
                    total = total + rr[c, d].astype(jnp.float32)
                if d < n_t - 1:
                    left_copy(c, d).wait_recv()
                    total = total + rl[c, d].astype(jnp.float32)
                out_ref[here] = total.astype(jnp.bfloat16)

    for distance in (4, 2):

        @pl.when(shard + distance < n_shards)
        def _():
            for i in range(2):
                kv_copy(i, distance).wait_send()

    for i in range(2):

        @pl.when(even)
        def _():
            fw_copy(i, 0, 1).wait_send()

        @pl.when(even & (shard >= 2))
        def _():
            fw_copy(i, 2, 3).wait_send()

        @pl.when(jnp.logical_not(even) & (shard >= 2))
        def _():
            fw_copy(i, 2, 1).wait_send()

        @pl.when(jnp.logical_not(even) & (shard >= 4))
        def _():
            fw_copy(i, 4, 3).wait_send()

        for distance in range(1, REACH + 1):

            @pl.when(shard >= distance)
            def _():
                if distance % 2:
                    pair_copy(i, distance).wait_send()
                else:
                    grad_copy(i, distance).wait_send()

    for c in range(CHUNKS):
        for d in range(n_t):

            @pl.when(t < d)
            def _():
                right_copy(c, d).wait_send()

            @pl.when(t > d)
            def _():
                left_copy(c, d).wait_send()


def hand_over(*refs):
    sources, targets, held, in_sem, out_sem = refs[:4], refs[4:8], refs[8:12], refs[12], refs[13]
    ins = [pltpu.make_async_copy(sources[i], held[i], in_sem.at[i]) for i in range(4)]
    outs = [pltpu.make_async_copy(held[i], targets[i], out_sem.at[i]) for i in range(4)]
    for c in ins:
        c.start()
    for i in range(4):
        ins[i].wait()
        outs[i].start()
    for c in outs:
        c.wait()


def shards(sizes, queries, keys, values, doc_lengths, w_out, d_out):
    n_t = sizes[2]
    rows, q_width = queries.shape
    kv_width = keys.shape[1]
    groups = kv_width // HEAD
    heads = q_width // HEAD
    per = heads // groups
    chunk = rows // CHUNKS
    ext = (REACH + 1) * rows
    window = REACH * rows + chunk
    d_model = w_out.shape[1]
    width = d_model // n_t
    bf, f32 = jnp.bfloat16, jnp.float32
    all_rows = per * rows
    n_w = 4
    anywhere = pl.BlockSpec(memory_space=pl.ANY)
    vmem = pl.BlockSpec(memory_space=pltpu.VMEM)
    dma = pltpu.SemaphoreType.DMA
    results = pl.pallas_call(
        functools.partial(kernel, sizes),
        out_shape=(
            jax.ShapeDtypeStruct((rows, width), bf),
            jax.ShapeDtypeStruct((rows, q_width), bf),
            jax.ShapeDtypeStruct((rows, kv_width), bf),
            jax.ShapeDtypeStruct((rows, kv_width), bf),
        ),
        in_specs=[
            anywhere, anywhere, anywhere, pl.BlockSpec(memory_space=pltpu.SMEM), anywhere, anywhere,
        ],
        out_specs=(vmem,) * 4,
        scratch_shapes=[
            pltpu.VMEM((rows, q_width), bf),
            pltpu.VMEM((rows, d_model), bf),
            pltpu.VMEM(w_out.shape, bf),
            pltpu.VMEM((ext, kv_width), bf),
            pltpu.VMEM((ext, kv_width), bf),
            pltpu.VMEM((groups, all_rows, HEAD), bf),
            pltpu.VMEM((groups, all_rows, HEAD), bf),
            pltpu.VMEM((CHUNKS, chunk, q_width), bf),
            pltpu.VMEM((CHUNKS, chunk, window), f32),
            pltpu.VMEM((per * chunk, window), f32),
            pltpu.VMEM((groups, all_rows, ext), bf),
            pltpu.VMEM((groups, all_rows, 1), f32),
            pltpu.VMEM((all_rows, rows), f32),
            pltpu.VMEM((all_rows, rows), bf),
            pltpu.VMEM((groups, all_rows, HEAD), f32),
            pltpu.VMEM((REACH, rows, kv_width), bf),
            pltpu.VMEM((REACH, rows, kv_width), bf),
            pltpu.VMEM((2, rows, kv_width), bf),
            pltpu.VMEM((2, rows, kv_width), bf),
            pltpu.VMEM((2, rows, kv_width), bf),
            pltpu.VMEM((2, rows, kv_width), bf),
            pltpu.VMEM((2, rows, kv_width), f32),
            pltpu.VMEM((CHUNKS, n_t, chunk, width), bf),
            pltpu.VMEM((CHUNKS, n_t, chunk, width), bf),
            pltpu.VMEM((CHUNKS, n_t, chunk, width), bf),
            dma((4,)),
            dma((n_w,)),
            dma((4,)),
            dma((4,)),
            dma((4,)),
            dma((4,)),
            dma((2, 2)),
            dma((2, 2)),
            dma((2, 2)),
            dma((2, 2)),
            dma((CHUNKS, n_t)),
            dma((CHUNKS, n_t)),
            dma((CHUNKS, n_t)),
            dma((CHUNKS, n_t)),
        ],
        compiler_params=pltpu.CompilerParams(
            collective_id=0, has_side_effects=True, vmem_limit_bytes=60 * 1024 * 1024
        ),
        name="layer",
    )(queries, keys, values, doc_lengths, w_out, d_out)
    return pl.pallas_call(
        hand_over,
        out_shape=tuple(jax.ShapeDtypeStruct(x.shape, x.dtype) for x in results),
        in_specs=[anywhere] * 4,
        out_specs=(anywhere,) * 4,
        scratch_shapes=[pltpu.VMEM(x.shape, x.dtype) for x in results] + [dma((4,)), dma((4,))],
        name="hand_over",
    )(*results)


def solution(mesh):
    sizes = tuple(mesh.shape[a] for a in ("seq", "server", "tensor"))
    tokens = P(("seq", "server"), "tensor")
    return jax.shard_map(
        functools.partial(shards, sizes),
        mesh=mesh,
        in_specs=(tokens, tokens, tokens, P(), P("tensor", None), P(("seq", "server"), None)),
        out_specs=(tokens,) * 4,
        check_vma=False,
    )
```
